256 devices in a mesh: dp: 64 (over x, z, core), proto: 4 (over y).
Axes of the slice: x: 4, y: 4, z: 8, core: 2. Of those that a mesh axis runs over, the one named last changes fastest.
Arguments:
- embeddings: bfloat16 [65536, 1024], P(('dp', 'proto')), may hold values from -6 to 6
- centres: bfloat16 [8192, 1024], P('proto'), may hold values from -0.1875 to 0.1875
Outputs:
- updated: bfloat16 [8192, 1024], P('proto')
The draws below stay inside these ranges and needn't reach their ends.
All inputs are finite; a program needn't handle non-finite values.
Results may differ from the reference program's by a relative error of at most 0.0074.
Values may be sent and summed in bfloat16 or wider, within the bound.
A program may use at most 64 MiB of HBM per device.

```python
import math
import jax
import jax.numpy as jnp
from jax import lax

D = 1024
K = 8192
ITERS = 3
ROWS = 65536


def block_scale(key, shape, cuts, low, largest):
    level, own = 1.0, jax.random.fold_in(key, 6)
    for dim, blocks in cuts:
        steps = jnp.exp(jax.random.uniform(jax.random.fold_in(own, dim), (blocks,), jnp.float32, low / len(cuts), largest / len(cuts)))
        level = level * jnp.repeat(steps, shape[dim] // blocks).reshape([-1 if axis == dim else 1 for axis in range(len(shape))])
    return level


def centred(key, shape, width, bound, cuts=(), dtype=jnp.bfloat16):
    array = jax.random.normal(key, shape, jnp.float32) * width
    if len(cuts) > 0:
        array = block_scale(key, shape, cuts, -0.22, 0.18) * array
    return jnp.clip(array, min=-bound, max=bound).astype(dtype)


def setup_inputs(seed: int = 0) -> dict:
    streams_of = jax.random.split(jax.random.key(seed), 3)
    return {
        "embeddings": centred(streams_of[0], (ROWS, D), 1.0, 6.0, ((0, 256),)),
        "centres": centred(streams_of[1], (K, D), D ** -0.5, 0.1875, ((0, 4),)),
    }


def normalise(rows):
    values = rows.astype(jnp.float32)
    scaled = values * lax.rsqrt(lax.optimization_barrier(jnp.mean(values * values, axis=1, keepdims=True)) + 1e-05)
    return scaled.astype(jnp.bfloat16)

def reference(embeddings, centres):
    unit = normalise(embeddings)
    block = math.gcd(ROWS, 1024)
    blocks = unit.reshape(ROWS // block, block, D)

    def score_block(rows):
        scores = lax.dot_general(rows, centres, (((1,), (1,)), ((), ())), preferred_element_type=jnp.float32)
        return jnp.exp(4.0 * scores)
    plan = lax.map(score_block, blocks).reshape(ROWS, K)
    for step in range(ITERS):
        colsum = lax.optimization_barrier(jnp.sum(plan, axis=0))
        plan = plan / (K * colsum)[None, :]
        rowsum = lax.optimization_barrier(jnp.sum(plan, axis=1))
        plan = plan / (ROWS * rowsum)[:, None]
    codes = (ROWS * plan).astype(jnp.bfloat16)
    sums = lax.dot_general(codes, unit, (((0,), (0,)), ((), ())), preferred_element_type=jnp.float32)
    updated = sums * lax.rsqrt(lax.optimization_barrier(jnp.mean(sums * sums, axis=1, keepdims=True)) + 1e-05)
    return updated.astype(jnp.bfloat16)
```

```python
import jax
import jax.numpy as jnp
from jax import lax
from jax.experimental import pallas as pl
from jax.experimental.pallas import tpu as pltpu
from jax.sharding import PartitionSpec as P

ITERS = 3
NX, NZ, NC, NY = 4, 8, 2, 4
F32, BF16 = jnp.float32, jnp.bfloat16
VMEM, DMA = pltpu.VMEM, pltpu.SemaphoreType.DMA


def remote(src, dst, send, recv, device):
    return pltpu.make_async_remote_copy(
        src_ref=src, dst_ref=dst, send_sem=send, recv_sem=recv,
        device_id=device, device_id_type=pl.DeviceIdType.MESH,
    )


def rescale(values):
    return values * lax.rsqrt(jnp.mean(values * values, axis=1, keepdims=True) + 1e-05)


class ScatterRing:
    def __init__(self, n, me, device, load, size, send, recv, ssem, rsem):
        self.n, self.me, self.device, self.load, self.size = n, me, device, load, size
        self.send_buf, self.recv_buf, self.ssem, self.rsem = send, recv, ssem, rsem
        self.half = send.shape[-1] // 2
        self.copies = {}

    def step(self, k):
        n, half, far = self.n, self.half, self.n // 2
        for d, sign in ((0, 1), (1, n - 1)):
            if k < far:
                self.copies[d, k + 1].wait_recv()
            block = lax.rem(self.me + (sign * k) % n, n)
            cols = pl.ds(d * half, half) if k == far else pl.ds(0, 2 * half)

            @pl.loop(0, self.size // 16)
            def _(i, d=d, block=block):
                rows = pl.ds(pl.multiple_of(i * 16, 16), 16)
                if k == far:
                    total = self.load(block, i, cols)
                    self.send_buf[d, k - 1, rows, cols] = total.astype(BF16)
                elif k == far - 1:
                    for h in range(2):
                        part = pl.ds(h * half, half)
                        total = self.load(block, i, part)
                        if h == d:
                            total = total + self.recv_buf[d, k, rows, part].astype(F32)
                        self.send_buf[d, k - 1, rows, part] = total.astype(BF16)
                else:
                    total = self.load(block, i, cols) + self.recv_buf[d, k, rows, :].astype(F32)
                    self.send_buf[d, k - 1, rows, :] = total.astype(BF16)

            copy = remote(
                self.send_buf.at[d, k - 1, :, cols], self.recv_buf.at[d, k - 1, :, cols],
                self.ssem.at[d, k - 1], self.rsem.at[d, k - 1],
                self.device(lax.rem(self.me + sign, n)),
            )
            copy.start()
            self.copies[d, k] = copy

    def finish(self, store):
        for d in range(2):
            self.copies[d, 1].wait_recv()

        @pl.loop(0, self.size // 16)
        def _(i):
            rows = pl.ds(pl.multiple_of(i * 16, 16), 16)
            total = self.load(self.me, i, pl.ds(0, 2 * self.half))
            for d in range(2):
                if self.n == 2 * 1:
                    continue
                total = total + self.recv_buf[d, 0, rows, :].astype(F32)
            store(i, total)

    def drain(self):
        for copy in self.copies.values():
            copy.wait_send()


class GatherRing:
    def __init__(self, n, me, device, base, size, out, ssem, rsem):
        self.n, self.me, self.device, self.base, self.size = n, me, device, base, size
        self.out, self.ssem, self.rsem = out, ssem, rsem
        self.half = out.shape[-1] // 2
        self.copies = {}

    def view(self, block, cols):
        start = pl.multiple_of(self.base + block * self.size, 16)
        return self.out.at[pl.ds(start, self.size), cols]

    def cols(self, d, k):
        return pl.ds(d * self.half, self.half) if k == self.n // 2 else pl.ds(0, 2 * self.half)

    def source(self, d, k):
        back = (self.n - k) % self.n if d == 0 else k % self.n
        return lax.rem(self.me + back, self.n)

    def step(self, k):
        for d, sign in ((0, 1), (1, self.n - 1)):
            view = self.view(self.source(d, k - 1), self.cols(d, k))
            copy = remote(
                view, view, self.ssem.at[d, k - 1], self.rsem.at[d, k - 1],
                self.device(lax.rem(self.me + sign, self.n)),
            )
            copy.start()
            self.copies[d, k] = copy

    def arrive(self, k):
        for d in range(2):
            self.copies[d, k].wait_recv()

    def drain(self):
        for copy in self.copies.values():
            copy.wait_send()


def kernel(
    emb_hbm, cen_hbm, out_hbm,
    emb, cen, unit, plan, scale_b, col_acc, row_scale,
    col_v, col_c, col_x, col_z, row_v, row_r,
    mate_s, mate_r, own, own_a, own_b,
    ax_s, ax_r, az_s, az_r, bz_s, bz_r, bx_s, bx_r, out,
    local_sem, unit_ss, unit_rs, col_ss, col_rs, row_ss, row_rs, mate_ss, mate_rs,
    ax_ss, ax_rs, az_ss, az_rs, bz_ss, bz_rs, bx_ss, bx_rs,
    gaz_ss, gaz_rs, gax_ss, gax_rs, gbx_ss, gbx_rs, gbz_ss, gbz_rs, fwd_ss, fwd_rs,
):
    rows, width = emb.shape
    protos = cen.shape[0]
    dp, y = lax.axis_index("dp"), lax.axis_index("proto")
    core = lax.rem(dp, NC)
    chip = lax.div(dp, NC)
    z, x = lax.rem(chip, NZ), lax.div(chip, NZ)
    mate = 1 - core

    def at(x, z, core):
        return ((x * NZ + z) * NC + core, y)

    def x_device(k):
        return at(k, z, core)

    def z_device(k):
        return at(x, k, core)

    mate_device = at(x, z, mate)
    x_peers = [x_device(lax.rem(x + k, NX)) for k in range(1, NX)]
    z_peers = [z_device(lax.rem(z + k, NZ)) for k in range(1, NZ)]
    y_peers = [(dp, lax.rem(y + k, NY)) for k in range(1, NY)]
    peers = [mate_device] + x_peers + z_peers + y_peers

    load_emb = pltpu.make_async_copy(emb_hbm, emb, local_sem.at[0])
    load_cen = pltpu.make_async_copy(cen_hbm, cen, local_sem.at[1])
    load_emb.start()
    load_cen.start()
    barrier = pltpu.get_barrier_semaphore()
    for peer in peers:
        pl.semaphore_signal(barrier, inc=1, device_id=peer, device_id_type=pl.DeviceIdType.MESH)
    load_emb.wait()

    @pl.loop(0, rows // 32)
    def _(i):
        part = pl.ds(pl.multiple_of(i * 32, 32), 32)
        unit[y, part, :] = rescale(emb[part, :].astype(F32)).astype(BF16)

    pl.semaphore_wait(barrier, len(peers))

    right, left, far = (lax.rem(y + k, NY) for k in (1, 3, 2))
    half = rows // 2

    def send_unit(index, block, which, to):
        view = unit.at[block, pl.ds(which * half, half), :]
        copy = remote(view, view, unit_ss.at[index], unit_rs.at[index], (dp, to))
        copy.start()
        return copy

    def scores(block, first):
        step = 256

        @pl.loop(0, protos // step)
        def _(i):
            js = pl.ds(pl.multiple_of(i * step, step), step)
            s = lax.dot_general(
                cen[js, :], unit[block], (((1,), (1,)), ((), ())), preferred_element_type=F32
            )
            p = jnp.exp(4.0 * s)
            plan[block, js, :] = p
            part = p[:, :128] + p[:, 128:]
            col_acc[js, :] = part if first else col_acc[js, :] + part

    ups = [send_unit(0, y, 0, right), send_unit(3, y, 1, left), send_unit(1, y, 1, right), send_unit(4, y, 0, left)]
    load_cen.wait()
    scores(y, True)
    ups[0].wait_recv()
    ups.append(send_unit(2, left, 0, right))
    ups[1].wait_recv()
    ups.append(send_unit(5, right, 1, left))
    ups[2].wait_recv()
    scores(left, False)
    ups[3].wait_recv()
    scores(right, False)
    ups[4].wait_recv()
    ups[5].wait_recv()
    scores(far, False)

    groups = protos // 128

    def lane_total(part):
        return jnp.sum(jnp.transpose(part), axis=0, keepdims=True)

    @pl.loop(0, groups)
    def _(g):
        col_v[0, 0, pl.ds(g, 1), :] = lane_total(col_acc[pl.ds(pl.multiple_of(g * 128, 128), 128), :])

    @pl.loop(0, ITERS)
    def _(t):
        copy = remote(col_v.at[t, 0], col_c.at[t], col_ss.at[t, 0], col_rs.at[t, 0], mate_device)
        copy.start()
        copy.wait()
        col_v[t, 1] = col_v[t, 0] + col_c[t]
        copies = [
            remote(col_v.at[t, 1], col_x.at[t, i], col_ss.at[t, 1 + i], col_rs.at[t, 1 + i], peer)
            for i, peer in enumerate(x_peers)
        ]
        for copy in copies:
            copy.start()
        for copy in copies:
            copy.wait()
        total = col_v[t, 1]
        for i in range(NX - 1):
            total = total + col_x[t, i]
        col_v[t, 2] = total
        copies = [
            remote(col_v.at[t, 2], col_z.at[t, i], col_ss.at[t, NX + i], col_rs.at[t, NX + i], peer)
            for i, peer in enumerate(z_peers)
        ]
        for copy in copies:
            copy.start()
        for copy in copies:
            copy.wait()
        total = col_v[t, 2]
        for i in range(NZ - 1):
            total = total + col_z[t, i]
        col_v[t, 3] = 1.0 / total

        def row_step(g, accs):
            js = pl.ds(pl.multiple_of(g * 128, 128), 128)
            spread = jnp.transpose(jnp.broadcast_to(col_v[t, 3, pl.ds(g, 1), :], (128, 128)))
            scale_b[js, :] = spread
            spread = jnp.concatenate([spread, spread], axis=1)
            return tuple(
                acc + jnp.sum((plan[b, js, :] * spread).reshape(16, 8, rows), axis=0)
                for b, acc in enumerate(accs)
            )

        accs = lax.fori_loop(0, groups, row_step, tuple(jnp.zeros((8, rows), F32) for _ in range(NY)))
        for b in range(NY):
            total = jnp.sum(accs[b], axis=0, keepdims=True)
            row_v[t, 2 * b : 2 * b + 1, :] = total[:, :128]
            row_v[t, 2 * b + 1 : 2 * b + 2, :] = total[:, 128:]
        copies = [
            remote(row_v.at[t], row_r.at[t, i], row_ss.at[t, i], row_rs.at[t, i], peer)
            for i, peer in enumerate(y_peers)
        ]
        for copy in copies:
            copy.start()
        for copy in copies:
            copy.wait()
        total = row_v[t]
        for i in range(NY - 1):
            total = total + row_r[t, i]
        row_scale[...] = 1.0 / total

        @pl.when(t < ITERS - 1)
        def _():
            @pl.loop(0, groups)
            def _(g):
                js = pl.ds(pl.multiple_of(g * 128, 128), 128)
                spread = scale_b[js, :]
                part = jnp.zeros((128, 128), F32)
                for b in range(NY):
                    for h in range(2):
                        lanes = pl.ds(h * 128, 128)
                        p = plan[b, js, lanes] * spread * row_scale[2 * b + h : 2 * b + h + 1, :]
                        plan[b, js, lanes] = p
                        part = part + p
                col_v[t + 1, 0, pl.ds(g, 1), :] = lane_total(part)

    step = 256
    mine = protos // 2
    all_unit = unit.reshape(NY * rows, width)

    def partial_sums(start):
        js = pl.ds(pl.multiple_of(start, step), step)
        spread = scale_b[js, :]
        codes = jnp.concatenate(
            [
                (plan[b, js, h * 128 : h * 128 + 128] * spread * row_scale[2 * b + h : 2 * b + h + 1, :]).astype(BF16)
                for b in range(NY)
                for h in range(2)
            ],
            axis=1,
        )
        return jnp.dot(codes, all_unit[...], preferred_element_type=F32)

    def mate_copy(q):
        view = pl.ds(pl.multiple_of(q * step, step), step)
        return remote(mate_s.at[view, :], mate_r.at[view, :], mate_ss.at[q], mate_rs.at[q], mate_device)

    @pl.loop(0, mine // step)
    def _(q):
        view = pl.ds(pl.multiple_of(q * step, step), step)
        mate_s[view, :] = partial_sums(mate * mine + q * step).astype(BF16)
        mate_copy(q).start()

    @pl.loop(0, mine // step)
    def _(q):
        view = pl.ds(pl.multiple_of(q * step, step), step)
        total = partial_sums(core * mine + q * step)
        mate_copy(q).wait_recv()
        own[view, :] = total + mate_r[view, :].astype(F32)

    part = mine // 2
    ax_size, bz_size = part // NX, part // NZ
    size = part // (NX * NZ)

    def loader(ref, base, size):
        def load(block, i, cols):
            return ref[pl.ds(pl.multiple_of(base + block * size + i * 16, 16), 16), cols]

        return load

    ax = ScatterRing(NX, x, x_device, loader(own, 0, ax_size), ax_size, ax_s, ax_r, ax_ss, ax_rs)
    bz = ScatterRing(NZ, z, z_device, loader(own, part, bz_size), bz_size, bz_s, bz_r, bz_ss, bz_rs)
    az = ScatterRing(NZ, z, z_device, loader(own_a, 0, size), size, az_s, az_r, az_ss, az_rs)
    bx = ScatterRing(NX, x, x_device, loader(own_b, 0, size), size, bx_s, bx_r, bx_ss, bx_rs)

    def keep(ref):
        def store(i, total):
            ref[pl.ds(pl.multiple_of(i * 16, 16), 16), :] = total

        return store

    def deliver(base):
        def store(i, total):
            out[pl.ds(pl.multiple_of(base + i * 16, 16), 16), :] = rescale(total).astype(BF16)

        return store

    base_a = core * mine
    base_b = base_a + part
    bz.step(4)
    ax.step(2)
    bz.step(3)
    ax.step(1)
    bz.step(2)
    bz.step(1)
    ax.finish(keep(own_a))
    az.step(4)
    bz.finish(keep(own_b))
    bx.step(2)
    az.step(3)
    bx.step(1)
    az.step(2)
    az.step(1)
    bx.finish(deliver(base_b + z * bz_size + x * size))
    gbx = GatherRing(NX, x, x_device, base_b + z * bz_size, size, out, gbx_ss, gbx_rs)
    gbx.step(1)
    az.finish(deliver(base_a + x * ax_size + z * size))
    gaz = GatherRing(NZ, z, z_device, base_a + x * ax_size, size, out, gaz_ss, gaz_rs)
    gaz.step(1)

    gax = GatherRing(NX, x, x_device, base_a, ax_size, out, gax_ss, gax_rs)
    gbz = GatherRing(NZ, z, z_device, base_b, bz_size, out, gbz_ss, gbz_rs)
    forwards = []

    def forward(view):
        index = len(forwards)
        copy = remote(view, view, fwd_ss.at[index], fwd_rs.at[index], mate_device)
        copy.start()
        forwards.append(copy)

    def forward_arrived(ring, k):
        ring.arrive(k)
        if k < ring.n // 2:
            ring.step(k + 1)
        for d in range(2):
            forward(ring.view(ring.source(d, k), ring.cols(d, k)))

    gbx.arrive(1)
    gbx.step(2)
    gaz.arrive(1)
    gaz.step(2)
    gbx.arrive(2)
    gbz.step(1)
    forward(gbz.view(z, pl.ds(0, width)))
    gaz.arrive(2)
    gaz.step(3)
    gaz.arrive(3)
    gaz.step(4)
    forward_arrived(gbz, 1)
    gaz.arrive(4)
    gax.step(1)
    forward(gax.view(x, pl.ds(0, width)))
    forward_arrived(gbz, 2)
    forward_arrived(gax, 1)
    forward_arrived(gbz, 3)
    forward_arrived(gax, 2)
    forward_arrived(gbz, 4)
    for copy in forwards:
        copy.wait_recv()
    store = pltpu.make_async_copy(out, out_hbm, local_sem.at[2])
    store.start()
    for copy in ups + forwards:
        copy.wait_send()
    for ring in (ax, bz, az, bx, gbx, gaz, gax, gbz):
        ring.drain()

    @pl.loop(0, mine // step)
    def _(q):
        mate_copy(q).wait_send()

    store.wait()


def per_device(embeddings, centres):
    rows, width = embeddings.shape
    protos = centres.shape[0]
    mine = protos // 2
    part = mine // 2
    ax_size, bz_size = part // NX, part // NZ
    size = part // (NX * NZ)
    rings = [(NX, ax_size), (NZ, size), (NZ, bz_size), (NX, size)]
    scratch = [
        VMEM((rows, width), BF16),
        VMEM((protos, width), BF16),
        VMEM((NY, rows, width), BF16),
        VMEM((NY, protos, rows), F32),
        VMEM((protos, 128), F32),
        VMEM((protos, 128), F32),
        VMEM((8, 128), F32),
        VMEM((ITERS, 4, protos // 128, 128), F32),
        VMEM((ITERS, protos // 128, 128), F32),
        VMEM((ITERS, NX - 1, protos // 128, 128), F32),
        VMEM((ITERS, NZ - 1, protos // 128, 128), F32),
        VMEM((ITERS, 8, 128), F32),
        VMEM((ITERS, NY - 1, 8, 128), F32),
        VMEM((mine, width), BF16),
        VMEM((mine, width), BF16),
        VMEM((mine, width), F32),
        VMEM((ax_size, width), F32),
        VMEM((bz_size, width), F32),
    ]
    for n, block in rings:
        scratch += [VMEM((2, n // 2, block, width), BF16)] * 2
    scratch += [VMEM((protos, width), BF16)]
    pairs = [(6,), (ITERS, 1 + NX - 1 + NZ - 1), (ITERS, NY - 1), (4,)]
    pairs += [(2, n // 2) for n, _ in rings]
    pairs += [(2, NZ // 2), (2, NX // 2), (2, NX // 2), (2, NZ // 2), (14,)]
    scratch += [DMA((3,))]
    for shape in pairs:
        scratch += [DMA(shape)] * 2
    return pl.pallas_call(
        kernel,
        out_shape=jax.ShapeDtypeStruct((protos, width), BF16),
        in_specs=[pl.BlockSpec(memory_space=pl.ANY)] * 2,
        out_specs=pl.BlockSpec(memory_space=pl.ANY),
        scratch_shapes=scratch,
        compiler_params=pltpu.CompilerParams(
            collective_id=0, has_side_effects=True, vmem_limit_bytes=60 * 1024 * 1024
        ),
    )(embeddings, centres)


def solution(mesh):
    return jax.shard_map(
        per_device,
        mesh=mesh,
        in_specs=(P(("dp", "proto"), None), P("proto", None)),
        out_specs=P("proto", None),
        check_vma=False,
    )
```

```python
import jax
import jax.numpy as jnp
from jax import lax
from jax.experimental import pallas as pl
from jax.experimental.pallas import tpu as pltpu
from jax.sharding import PartitionSpec as P

ITERS = 3
NX, NZ, NC, NY = 4, 8, 2, 4
WINDOWS = 2
F32, BF16 = jnp.float32, jnp.bfloat16
VMEM, DMA = pltpu.VMEM, pltpu.SemaphoreType.DMA


def remote(src, dst, send, recv, device):
    return pltpu.make_async_remote_copy(
        src_ref=src, dst_ref=dst, send_sem=send, recv_sem=recv,
        device_id=device, device_id_type=pl.DeviceIdType.MESH,
    )


def rescale(values):
    return values * lax.rsqrt(jnp.mean(values * values, axis=1, keepdims=True) + 1e-05)


class ScatterRing:
    def __init__(self, n, me, device, load, size, send, recv, ssem, rsem, window):
        self.n, self.me, self.device, self.load, self.size = n, me, device, load, size
        self.send_buf, self.recv_buf, self.ssem, self.rsem = send, recv, ssem, rsem
        self.window, self.start, self.width = window
        self.copies = {}

    def step(self, k):
        far, half = self.n // 2, self.width // 2
        everything = pl.ds(self.start, self.width)
        for d, sign in ((0, 1), (1, -1)):
            if k < far:
                self.copies[d, k + 1].wait_recv()
            mine = pl.ds(self.start + d * half, half)
            other = pl.ds(self.start + (1 - d) * half, half)

            @pl.loop(0, self.size // 16)
            def _(i, d=d, sign=sign):
                rows = pl.ds(pl.multiple_of(i * 16, 16), 16)

                def put(cols, add):
                    total = self.load(sign * k, i, cols)
                    if add:
                        total = total + self.recv_buf[d, k, rows, cols].astype(F32)
                    self.send_buf[d, k - 1, rows, cols] = total.astype(BF16)

                if k == far:
                    put(mine, False)
                elif k == far - 1:
                    put(mine, True)
                    put(other, False)
                else:
                    put(everything, True)

            cols = mine if k == far else everything
            copy = remote(
                self.send_buf.at[d, k - 1, :, cols], self.recv_buf.at[d, k - 1, :, cols],
                self.ssem.at[self.window, d, k - 1], self.rsem.at[self.window, d, k - 1],
                self.device(lax.rem(self.me + sign + self.n, self.n)),
            )
            copy.start()
            self.copies[d, k] = copy

    def finish(self, store):
        cols = pl.ds(self.start, self.width)
        for d in range(2):
            self.copies[d, 1].wait_recv()

        @pl.loop(0, self.size // 16)
        def _(i):
            rows = pl.ds(pl.multiple_of(i * 16, 16), 16)
            total = self.load(0, i, cols)
            for d in range(2):
                total = total + self.recv_buf[d, 0, rows, cols].astype(F32)
            store(i, cols, total)

    def drain(self):
        for copy in self.copies.values():
            copy.wait_send()


class GatherRing:
    def __init__(self, n, me, device, base, size, out, ssem, rsem, window):
        self.n, self.me, self.device, self.base, self.size = n, me, device, base, size
        self.out, self.ssem, self.rsem = out, ssem, rsem
        self.window, self.start, self.width = window
        self.copies = {}

    def view(self, block, cols):
        start = pl.multiple_of(self.base + block * self.size, 16)
        return self.out.at[pl.ds(start, self.size), cols]

    def cols(self, d, k):
        half = self.width // 2
        return pl.ds(self.start + d * half, half) if k == self.n // 2 else pl.ds(self.start, self.width)

    def source(self, d, k):
        back = (self.n - k) % self.n if d == 0 else k % self.n
        return lax.rem(self.me + back, self.n)

    def step(self, k):
        for d, sign in ((0, 1), (1, self.n - 1)):
            view = self.view(self.source(d, k - 1), self.cols(d, k))
            copy = remote(
                view, view, self.ssem.at[self.window, d, k - 1], self.rsem.at[self.window, d, k - 1],
                self.device(lax.rem(self.me + sign, self.n)),
            )
            copy.start()
            self.copies[d, k] = copy

    def arrive(self, k):
        for d in range(2):
            self.copies[d, k].wait_recv()

    def drain(self):
        for copy in self.copies.values():
            copy.wait_send()


def kernel(
    emb_hbm, cen_hbm, out,
    emb, cen, unit, plan, scale_b, col_acc, row_scale,
    col_v, col_c, col_x, col_z, row_v, row_r,
    mate_s, mate_r, own, own_a, own_b,
    ax_s, ax_r, az_s, az_r, bz_s, bz_r, bx_s, bx_r,
    local_sem, unit_ss, unit_rs, col_ss, col_rs, row_ss, row_rs, mate_ss, mate_rs,
    ax_ss, ax_rs, az_ss, az_rs, bz_ss, bz_rs, bx_ss, bx_rs,
    gaz_ss, gaz_rs, gax_ss, gax_rs, gbx_ss, gbx_rs, gbz_ss, gbz_rs, fwd_ss, fwd_rs,
):
    rows, width = emb.shape
    protos = cen.shape[0]
    dp, y = lax.axis_index("dp"), lax.axis_index("proto")
    core = lax.rem(dp, NC)
    chip = lax.div(dp, NC)
    z, x = lax.rem(chip, NZ), lax.div(chip, NZ)
    mate = 1 - core

    def at(x, z, core):
        return ((x * NZ + z) * NC + core, y)

    def x_device(k):
        return at(k, z, core)

    def z_device(k):
        return at(x, k, core)

    mate_device = at(x, z, mate)
    x_peers = [x_device(lax.rem(x + k, NX)) for k in range(1, NX)]
    z_peers = [z_device(lax.rem(z + k, NZ)) for k in range(1, NZ)]
    y_peers = [(dp, lax.rem(y + k, NY)) for k in range(1, NY)]
    peers = [mate_device] + x_peers + z_peers + y_peers

    load_emb = pltpu.make_async_copy(emb_hbm, emb, local_sem.at[0])
    load_cen = pltpu.make_async_copy(cen_hbm, cen, local_sem.at[1])
    load_emb.start()
    load_cen.start()
    barrier = pltpu.get_barrier_semaphore()
    for peer in peers:
        pl.semaphore_signal(barrier, inc=1, device_id=peer, device_id_type=pl.DeviceIdType.MESH)
    load_emb.wait()

    @pl.loop(0, rows // 32)
    def _(i):
        part = pl.ds(pl.multiple_of(i * 32, 32), 32)
        unit[y, part, :] = rescale(emb[part, :].astype(F32)).astype(BF16)

    pl.semaphore_wait(barrier, len(peers))

    right, left, far = (lax.rem(y + k, NY) for k in (1, 3, 2))
    half = rows // 2

    def send_unit(index, block, which, to):
        view = unit.at[block, pl.ds(which * half, half), :]
        copy = remote(view, view, unit_ss.at[index], unit_rs.at[index], (dp, to))
        copy.start()
        return copy

    def scores(block, first):
        step = 256

        @pl.loop(0, protos // step)
        def _(i):
            js = pl.ds(pl.multiple_of(i * step, step), step)
            s = lax.dot_general(
                cen[js, :], unit[block], (((1,), (1,)), ((), ())), preferred_element_type=F32
            )
            p = jnp.exp(4.0 * s)
            plan[block, js, :] = p
            part = p[:, :128] + p[:, 128:]
            col_acc[js, :] = part if first else col_acc[js, :] + part

    ups = [send_unit(0, y, 0, right), send_unit(3, y, 1, left), send_unit(1, y, 1, right), send_unit(4, y, 0, left)]
    load_cen.wait()
    scores(y, True)
    ups[0].wait_recv()
    ups.append(send_unit(2, left, 0, right))
    ups[1].wait_recv()
    ups.append(send_unit(5, right, 1, left))
    ups[2].wait_recv()
    scores(left, False)
    ups[3].wait_recv()
    scores(right, False)
    ups[4].wait_recv()
    ups[5].wait_recv()
    scores(far, False)

    groups = protos // 128

    def lane_total(part):
        return jnp.sum(jnp.transpose(part), axis=0, keepdims=True)

    @pl.loop(0, groups)
    def _(g):
        col_v[0, 0, pl.ds(g, 1), :] = lane_total(col_acc[pl.ds(pl.multiple_of(g * 128, 128), 128), :])

    @pl.loop(0, ITERS)
    def _(t):
        copy = remote(col_v.at[t, 0], col_c.at[t], col_ss.at[t, 0], col_rs.at[t, 0], mate_device)
        copy.start()
        copy.wait()
        col_v[t, 1] = col_v[t, 0] + col_c[t]
        copies = [
            remote(col_v.at[t, 1], col_x.at[t, i], col_ss.at[t, 1 + i], col_rs.at[t, 1 + i], peer)
            for i, peer in enumerate(x_peers)
        ]
        for copy in copies:
            copy.start()
        for copy in copies:
            copy.wait()
        total = col_v[t, 1]
        for i in range(NX - 1):
            total = total + col_x[t, i]
        col_v[t, 2] = total
        copies = [
            remote(col_v.at[t, 2], col_z.at[t, i], col_ss.at[t, NX + i], col_rs.at[t, NX + i], peer)
            for i, peer in enumerate(z_peers)
        ]
        for copy in copies:
            copy.start()
        for copy in copies:
            copy.wait()
        total = col_v[t, 2]
        for i in range(NZ - 1):
            total = total + col_z[t, i]
        col_v[t, 3] = 1.0 / total

        def row_step(g, accs):
            js = pl.ds(pl.multiple_of(g * 128, 128), 128)
            spread = jnp.transpose(jnp.broadcast_to(col_v[t, 3, pl.ds(g, 1), :], (128, 128)))
            scale_b[js, :] = spread
            spread = jnp.concatenate([spread, spread], axis=1)
            return tuple(
                acc + jnp.sum((plan[b, js, :] * spread).reshape(16, 8, rows), axis=0)
                for b, acc in enumerate(accs)
            )

        accs = lax.fori_loop(0, groups, row_step, tuple(jnp.zeros((8, rows), F32) for _ in range(NY)))
        for b in range(NY):
            total = jnp.sum(accs[b], axis=0, keepdims=True)
            row_v[t, 2 * b : 2 * b + 1, :] = total[:, :128]
            row_v[t, 2 * b + 1 : 2 * b + 2, :] = total[:, 128:]
        copies = [
            remote(row_v.at[t], row_r.at[t, i], row_ss.at[t, i], row_rs.at[t, i], peer)
            for i, peer in enumerate(y_peers)
        ]
        for copy in copies:
            copy.start()
        for copy in copies:
            copy.wait()
        total = row_v[t]
        for i in range(NY - 1):
            total = total + row_r[t, i]
        row_scale[...] = 1.0 / total

        @pl.when(t < ITERS - 1)
        def _():
            @pl.loop(0, groups)
            def _(g):
                js = pl.ds(pl.multiple_of(g * 128, 128), 128)
                spread = scale_b[js, :]
                part = jnp.zeros((128, 128), F32)
                for b in range(NY):
                    for h in range(2):
                        lanes = pl.ds(h * 128, 128)
                        p = plan[b, js, lanes] * spread * row_scale[2 * b + h : 2 * b + h + 1, :]
                        plan[b, js, lanes] = p
                        part = part + p
                col_v[t + 1, 0, pl.ds(g, 1), :] = lane_total(part)

    mine = protos // 2
    part = mine // 2
    ax_size, bz_size = part // NX, part // NZ
    size = part // (NX * NZ)
    all_unit = unit.reshape(NY * rows, width)
    order = [(4, 3, 2), (-3, 2, 1), (-2, 1, -1), (-1, 0, 0)]

    def codes(start, count):
        js = pl.ds(pl.multiple_of(start, 64), count)
        spread = scale_b[js, :]
        return jnp.concatenate(
            [
                (plan[b, js, h * 128 : h * 128 + 128] * spread * row_scale[2 * b + h : 2 * b + h + 1, :]).astype(BF16)
                for b in range(NY)
                for h in range(2)
            ],
            axis=1,
        )

    def partial_sums(base, s):
        first, second, third = order[s]
        lhs = [
            codes(base + part + lax.rem(z + first + NZ, NZ) * bz_size, bz_size),
            codes(base + part + lax.rem(z + second + NZ, NZ) * bz_size, bz_size),
            codes(base + lax.rem(x + third + NX, NX) * ax_size, ax_size),
        ]
        return jnp.dot(jnp.concatenate(lhs, axis=0), all_unit[...], preferred_element_type=F32)

    mate_copies = []

    def sums(s):
        mate_s[s] = partial_sums(mate * mine, s).astype(BF16)
        copy = remote(mate_s.at[s], mate_r.at[s], mate_ss.at[s], mate_rs.at[s], mate_device)
        copy.start()
        mate_copies.append(copy)
        total = partial_sums(core * mine, s)
        copy.wait_recv()
        own[s] = total + mate_r[s].astype(F32)

    place_b = {off: (s, i * bz_size) for s, row in enumerate(order) for i, off in enumerate(row[:2])}
    place_a = {row[2]: (s, 2 * bz_size) for s, row in enumerate(order)}

    def load_b(off, i, cols):
        s, start = place_b[off if off in place_b else off + NZ]
        return own[s, pl.ds(pl.multiple_of(start + i * 16, 16), 16), cols]

    def load_a(off, i, cols):
        s, start = place_a[off if off in place_a else off + NX]
        return own[s, pl.ds(pl.multiple_of(start + i * 16, 16), 16), cols]

    def loader(ref, me, n):
        def load(off, i, cols):
            block = lax.rem(me + off + n, n)
            return ref[pl.ds(pl.multiple_of(block * size + i * 16, 16), 16), cols]

        return load

    whole = (0, 0, width)
    windows = [(w, w * (width // WINDOWS), width // WINDOWS) for w in range(WINDOWS)]
    ax = [ScatterRing(NX, x, x_device, load_a, ax_size, ax_s, ax_r, ax_ss, ax_rs, w) for w in windows]
    bz = [ScatterRing(NZ, z, z_device, load_b, bz_size, bz_s, bz_r, bz_ss, bz_rs, w) for w in windows]
    az = ScatterRing(NZ, z, z_device, loader(own_a, z, NZ), size, az_s, az_r, az_ss, az_rs, whole)
    bx = ScatterRing(NX, x, x_device, loader(own_b, x, NX), size, bx_s, bx_r, bx_ss, bx_rs, whole)

    def keep(ref):
        def store(i, cols, total):
            ref[pl.ds(pl.multiple_of(i * 16, 16), 16), cols] = total

        return store

    def deliver(base):
        def store(i, cols, total):
            out[pl.ds(pl.multiple_of(base + i * 16, 16), 16), :] = rescale(total).astype(BF16)

        return store

    def each(rings, k):
        for ring in rings:
            ring.step(k)

    base_a = core * mine
    base_b = base_a + part
    sums(0)
    each(bz, 4)
    each(ax, 2)
    sums(1)
    each(bz, 3)
    sums(2)
    each(ax, 1)
    sums(3)
    each(bz, 2)
    each(bz, 1)
    for ring in ax:
        ring.finish(keep(own_a))
    az.step(4)
    for ring in bz:
        ring.finish(keep(own_b))
    bx.step(2)
    az.step(3)
    bx.step(1)
    az.step(2)
    bx.finish(deliver(base_b + z * bz_size + x * size))
    gbx = GatherRing(NX, x, x_device, base_b + z * bz_size, size, out, gbx_ss, gbx_rs, whole)
    gbx.step(1)
    az.step(1)
    gbx.arrive(1)
    gbx.step(2)
    az.finish(deliver(base_a + x * ax_size + z * size))
    gaz = GatherRing(NZ, z, z_device, base_a + x * ax_size, size, out, gaz_ss, gaz_rs, whole)
    gaz.step(1)

    gax = [GatherRing(NX, x, x_device, base_a, ax_size, out, gax_ss, gax_rs, w) for w in windows]
    gbz = [GatherRing(NZ, z, z_device, base_b, bz_size, out, gbz_ss, gbz_rs, w) for w in windows]
    forwards = []

    def forward(view):
        index = len(forwards)
        copy = remote(view, view, fwd_ss.at[index], fwd_rs.at[index], mate_device)
        copy.start()
        forwards.append(copy)

    def arrived(ring, k):
        ring.arrive(k)
        if k < ring.n // 2:
            ring.step(k + 1)
        for d in range(2):
            forward(ring.view(ring.source(d, k), ring.cols(d, k)))

    gbx.arrive(2)
    each(gbz, 1)
    forward(gbz[0].view(z, pl.ds(0, width)))
    gaz.arrive(1)
    gaz.step(2)
    gaz.arrive(2)
    gaz.step(3)
    arrived(gbz[0], 1)
    gaz.arrive(3)
    gaz.step(4)
    for ring in gbz[1:]:
        arrived(ring, 1)
    gaz.arrive(4)
    each(gax, 1)
    forward(gax[0].view(x, pl.ds(0, width)))
    for rings, k in ((gbz, 2), (gax, 1), (gbz, 3), (gax, 2), (gbz, 4)):
        for ring in rings:
            arrived(ring, k)
    for copy in forwards:
        copy.wait_recv()
    for copy in ups + forwards + mate_copies:
        copy.wait_send()
    for ring in ax + bz + [az, bx, gbx, gaz] + gax + gbz:
        ring.drain()


def per_device(embeddings, centres):
    rows, width = embeddings.shape
    protos = centres.shape[0]
    mine = protos // 2
    part = mine // 2
    ax_size, bz_size = part // NX, part // NZ
    size = part // (NX * NZ)
    rings = [(NX, ax_size), (NZ, size), (NZ, bz_size), (NX, size)]
    scratch = [
        VMEM((rows, width), BF16),
        VMEM((protos, width), BF16),
        VMEM((NY, rows, width), BF16),
        VMEM((NY, protos, rows), F32),
        VMEM((protos, 128), F32),
        VMEM((protos, 128), F32),
        VMEM((8, 128), F32),
        VMEM((ITERS, 4, protos // 128, 128), F32),
        VMEM((ITERS, protos // 128, 128), F32),
        VMEM((ITERS, NX - 1, protos // 128, 128), F32),
        VMEM((ITERS, NZ - 1, protos // 128, 128), F32),
        VMEM((ITERS, 8, 128), F32),
        VMEM((ITERS, NY - 1, 8, 128), F32),
        VMEM((4, mine // 4, width), BF16),
        VMEM((4, mine // 4, width), BF16),
        VMEM((4, mine // 4, width), F32),
        VMEM((ax_size, width), F32),
        VMEM((bz_size, width), F32),
    ]
    for n, block in rings:
        scratch += [VMEM((2, n // 2, block, width), BF16)] * 2
    pairs = [(6,), (ITERS, 1 + NX - 1 + NZ - 1), (ITERS, NY - 1), (4,)]
    counts = [WINDOWS, 1, WINDOWS, 1]
    pairs += [(w, 2, n // 2) for (n, _), w in zip(rings, counts)]
    pairs += [(1, 2, NZ // 2), (WINDOWS, 2, NX // 2), (1, 2, NX // 2), (WINDOWS, 2, NZ // 2)]
    pairs += [(2 + WINDOWS * (NX + NZ),)]
    scratch += [DMA((2,))]
    for shape in pairs:
        scratch += [DMA(shape)] * 2
    return pl.pallas_call(
        kernel,
        out_shape=VMEM((protos, width), BF16),
        in_specs=[pl.BlockSpec(memory_space=pltpu.HBM)] * 2,
        out_specs=pl.BlockSpec(memory_space=pltpu.VMEM),
        scratch_shapes=scratch,
        compiler_params=pltpu.CompilerParams(
            collective_id=0, has_side_effects=True, vmem_limit_bytes=56 * 1024 * 1024
        ),
    )(embeddings, centres)


def solution(mesh):
    return jax.shard_map(
        per_device,
        mesh=mesh,
        in_specs=(P(("dp", "proto"), None), P("proto", None)),
        out_specs=P("proto", None),
        check_vma=False,
    )
```

```python
import jax
import jax.numpy as jnp
from jax import lax
from jax.experimental import pallas as pl
from jax.experimental.pallas import tpu as pltpu
from jax.sharding import PartitionSpec as P

ITERS = 3
NX, NZ, NC, NY = 4, 8, 2, 4
WINDOWS = 2
F32, BF16 = jnp.float32, jnp.bfloat16
VMEM, DMA = pltpu.VMEM, pltpu.SemaphoreType.DMA


def remote(src, dst, send, recv, device):
    return pltpu.make_async_remote_copy(
        src_ref=src, dst_ref=dst, send_sem=send, recv_sem=recv,
        device_id=device, device_id_type=pl.DeviceIdType.MESH,
    )


def rescale(values):
    return values * lax.rsqrt(jnp.mean(values * values, axis=1, keepdims=True) + 1e-05)


class ScatterRing:
    def __init__(self, n, me, device, load, size, send, recv, ssem, rsem, window):
        self.n, self.me, self.device, self.load, self.size = n, me, device, load, size
        self.send_buf, self.recv_buf, self.ssem, self.rsem = send, recv, ssem, rsem
        self.window, self.start, self.width = window
        self.copies = {}

    def step(self, k):
        far, half = self.n // 2, self.width // 2
        everything = pl.ds(self.start, self.width)
        for d, sign in ((0, 1), (1, -1)):
            if k < far:
                self.copies[d, k + 1].wait_recv()
            mine = pl.ds(self.start + d * half, half)
            other = pl.ds(self.start + (1 - d) * half, half)

            @pl.loop(0, self.size // 16)
            def _(i, d=d, sign=sign):
                rows = pl.ds(pl.multiple_of(i * 16, 16), 16)

                def put(cols, add):
                    total = self.load(sign * k, i, cols)
                    if add:
                        total = total + self.recv_buf[d, k, rows, cols].astype(F32)
                    self.send_buf[d, k - 1, rows, cols] = total.astype(BF16)

                if k == far:
                    put(mine, False)
                elif k == far - 1:
                    put(mine, True)
                    put(other, False)
                else:
                    put(everything, True)

            cols = mine if k == far else everything
            copy = remote(
                self.send_buf.at[d, k - 1, :, cols], self.recv_buf.at[d, k - 1, :, cols],
                self.ssem.at[self.window, d, k - 1], self.rsem.at[self.window, d, k - 1],
                self.device(lax.rem(self.me + sign + self.n, self.n)),
            )
            copy.start()
            self.copies[d, k] = copy

    def finish(self, store):
        cols = pl.ds(self.start, self.width)
        for d in range(2):
            self.copies[d, 1].wait_recv()

        @pl.loop(0, self.size // 16)
        def _(i):
            rows = pl.ds(pl.multiple_of(i * 16, 16), 16)
            total = self.load(0, i, cols)
            for d in range(2):
                total = total + self.recv_buf[d, 0, rows, cols].astype(F32)
            store(i, cols, total)

    def drain(self):
        for copy in self.copies.values():
            copy.wait_send()


class GatherRing:
    def __init__(self, n, me, device, base, size, out, ssem, rsem, window):
        self.n, self.me, self.device, self.base, self.size = n, me, device, base, size
        self.out, self.ssem, self.rsem = out, ssem, rsem
        self.window, self.start, self.width = window
        self.copies = {}

    def view(self, block, cols):
        start = pl.multiple_of(self.base + block * self.size, 16)
        return self.out.at[pl.ds(start, self.size), cols]

    def cols(self, d, k):
        half = self.width // 2
        return pl.ds(self.start + d * half, half) if k == self.n // 2 else pl.ds(self.start, self.width)

    def source(self, d, k):
        back = (self.n - k) % self.n if d == 0 else k % self.n
        return lax.rem(self.me + back, self.n)

    def step(self, k):
        for d, sign in ((0, 1), (1, self.n - 1)):
            view = self.view(self.source(d, k - 1), self.cols(d, k))
            copy = remote(
                view, view, self.ssem.at[self.window, d, k - 1], self.rsem.at[self.window, d, k - 1],
                self.device(lax.rem(self.me + sign, self.n)),
            )
            copy.start()
            self.copies[d, k] = copy

    def arrive(self, k):
        for d in range(2):
            self.copies[d, k].wait_recv()

    def drain(self):
        for copy in self.copies.values():
            copy.wait_send()


def kernel(
    emb_hbm, cen_hbm, out,
    emb, cen, unit, plan, scale_b, col_acc, row_scale,
    col_v, col_c, col_x, col_z, row_v, row_r,
    mate_s, mate_r, own, own_a, own_b,
    ax_s, ax_r, az_s, az_r, bz_s, bz_r, bx_s, bx_r,
    local_sem, unit_ss, unit_rs, col_ss, col_rs, row_ss, row_rs, mate_ss, mate_rs,
    ax_ss, ax_rs, az_ss, az_rs, bz_ss, bz_rs, bx_ss, bx_rs,
    gaz_ss, gaz_rs, gax_ss, gax_rs, gbx_ss, gbx_rs, gbz_ss, gbz_rs, fwd_ss, fwd_rs,
):
    rows, width = emb.shape
    protos = cen.shape[0]
    dp, y = lax.axis_index("dp"), lax.axis_index("proto")
    core = lax.rem(dp, NC)
    chip = lax.div(dp, NC)
    z, x = lax.rem(chip, NZ), lax.div(chip, NZ)
    mate = 1 - core

    def at(x, z, core):
        return ((x * NZ + z) * NC + core, y)

    def x_device(k):
        return at(k, z, core)

    def z_device(k):
        return at(x, k, core)

    mate_device = at(x, z, mate)
    x_peers = [x_device(lax.rem(x + k, NX)) for k in (2, 1, 3)]
    z_peers = [z_device(lax.rem(z + k, NZ)) for k in (4, 3, 5, 2, 6, 1, 7)]
    y_peers = [(dp, lax.rem(y + k, NY)) for k in (2, 1, 3)]
    peers = [mate_device] + x_peers + z_peers + y_peers

    load_emb = pltpu.make_async_copy(emb_hbm, emb, local_sem.at[0])
    load_cen = pltpu.make_async_copy(cen_hbm, cen, local_sem.at[1])
    load_emb.start()
    load_cen.start()
    barrier = pltpu.get_barrier_semaphore()
    for peer in peers:
        pl.semaphore_signal(barrier, inc=1, device_id=peer, device_id_type=pl.DeviceIdType.MESH)
    load_emb.wait()

    @pl.loop(0, rows // 32)
    def _(i):
        part = pl.ds(pl.multiple_of(i * 32, 32), 32)
        unit[y, part, :] = rescale(emb[part, :].astype(F32)).astype(BF16)

    pl.semaphore_wait(barrier, len(peers))

    right, left, far = (lax.rem(y + k, NY) for k in (1, 3, 2))
    half = rows // 2

    def send_unit(index, block, which, to):
        view = unit.at[block, pl.ds(which * half, half), :]
        copy = remote(view, view, unit_ss.at[index], unit_rs.at[index], (dp, to))
        copy.start()
        return copy

    def scores(block, first):
        step = 1024

        @pl.loop(0, protos // step)
        def _(i):
            js = pl.ds(pl.multiple_of(i * step, step), step)
            s = lax.dot_general(
                cen[js, :], unit[block], (((1,), (1,)), ((), ())), preferred_element_type=F32
            )
            p = jnp.exp(4.0 * s)
            plan[block, js, :] = p
            part = p[:, :128] + p[:, 128:]
            col_acc[js, :] = part if first else col_acc[js, :] + part

    ups = [send_unit(0, y, 0, right), send_unit(3, y, 1, left), send_unit(1, y, 1, right), send_unit(4, y, 0, left)]
    load_cen.wait()
    scores(y, True)
    ups[0].wait_recv()
    ups.append(send_unit(2, left, 0, right))
    ups[1].wait_recv()
    ups.append(send_unit(5, right, 1, left))
    ups[2].wait_recv()
    scores(left, False)
    ups[3].wait_recv()
    scores(right, False)
    ups[4].wait_recv()
    ups[5].wait_recv()
    scores(far, False)

    groups = protos // 128

    def lane_total(part):
        return jnp.sum(jnp.transpose(part), axis=0, keepdims=True)

    @pl.loop(0, groups)
    def _(g):
        col_v[0, 0, pl.ds(g, 1), :] = lane_total(col_acc[pl.ds(pl.multiple_of(g * 128, 128), 128), :])

    @pl.loop(0, ITERS)
    def _(t):
        copy = remote(col_v.at[t, 0], col_c.at[t], col_ss.at[t, 0], col_rs.at[t, 0], mate_device)
        copy.start()
        copy.wait()
        col_v[t, 1] = col_v[t, 0] + col_c[t]
        copies = [
            remote(col_v.at[t, 1], col_x.at[t, i], col_ss.at[t, 1 + i], col_rs.at[t, 1 + i], peer)
            for i, peer in enumerate(x_peers)
        ]
        for copy in copies:
            copy.start()
        for copy in copies:
            copy.wait()
        total = col_v[t, 1]
        for i in range(NX - 1):
            total = total + col_x[t, i]
        col_v[t, 2] = total
        copies = [
            remote(col_v.at[t, 2], col_z.at[t, i], col_ss.at[t, NX + i], col_rs.at[t, NX + i], peer)
            for i, peer in enumerate(z_peers)
        ]
        for copy in copies:
            copy.start()
        for copy in copies:
            copy.wait()
        total = col_v[t, 2]
        for i in range(NZ - 1):
            total = total + col_z[t, i]
        col_v[t, 3] = 1.0 / total

        def row_step(g, accs):
            js = pl.ds(pl.multiple_of(g * 128, 128), 128)
            spread = jnp.transpose(jnp.broadcast_to(col_v[t, 3, pl.ds(g, 1), :], (128, 128)))
            scale_b[js, :] = spread
            spread = jnp.concatenate([spread, spread], axis=1)
            return tuple(
                acc + jnp.sum((plan[b, js, :] * spread).reshape(16, 8, rows), axis=0)
                for b, acc in enumerate(accs)
            )

        accs = lax.fori_loop(0, groups, row_step, tuple(jnp.zeros((8, rows), F32) for _ in range(NY)))
        for b in range(NY):
            total = jnp.sum(accs[b], axis=0, keepdims=True)
            row_v[t, 2 * b : 2 * b + 1, :] = total[:, :128]
            row_v[t, 2 * b + 1 : 2 * b + 2, :] = total[:, 128:]
        copies = [
            remote(row_v.at[t], row_r.at[t, i], row_ss.at[t, i], row_rs.at[t, i], peer)
            for i, peer in enumerate(y_peers)
        ]
        for copy in copies:
            copy.start()
        for copy in copies:
            copy.wait()
        total = row_v[t]
        for i in range(NY - 1):
            total = total + row_r[t, i]
        row_scale[...] = 1.0 / total

        @pl.when(t < ITERS - 1)
        def _():
            @pl.loop(0, groups)
            def _(g):
                js = pl.ds(pl.multiple_of(g * 128, 128), 128)
                spread = scale_b[js, :]
                part = jnp.zeros((128, 128), F32)
                for b in range(NY):
                    for h in range(2):
                        lanes = pl.ds(h * 128, 128)
                        p = plan[b, js, lanes] * spread * row_scale[2 * b + h : 2 * b + h + 1, :]
                        plan[b, js, lanes] = p
                        part = part + p
                col_v[t + 1, 0, pl.ds(g, 1), :] = lane_total(part)

    mine = protos // 2
    part = mine // 2
    ax_size, bz_size = part // NX, part // NZ
    size = part // (NX * NZ)
    all_unit = unit.reshape(NY * rows, width)
    order = [(4, 3, 2), (-3, 2, 1), (-2, 1, -1), (-1, 0, 0)]

    def codes(start, count):
        js = pl.ds(pl.multiple_of(start, 64), count)
        spread = scale_b[js, :]
        return jnp.concatenate(
            [
                (plan[b, js, h * 128 : h * 128 + 128] * spread * row_scale[2 * b + h : 2 * b + h + 1, :]).astype(BF16)
                for b in range(NY)
                for h in range(2)
            ],
            axis=1,
        )

    def partial_sums(base, s):
        first, second, third = order[s]
        lhs = [
            codes(base + part + lax.rem(z + first + NZ, NZ) * bz_size, bz_size),
            codes(base + part + lax.rem(z + second + NZ, NZ) * bz_size, bz_size),
            codes(base + lax.rem(x + third + NX, NX) * ax_size, ax_size),
        ]
        return jnp.dot(jnp.concatenate(lhs, axis=0), all_unit[...], preferred_element_type=F32)

    def mate_copy(s):
        return remote(mate_s.at[s], mate_r.at[s], mate_ss.at[s], mate_rs.at[s], mate_device)

    def sums(s):
        @pl.when(core < NC)
        def _():
            mate_s[s] = partial_sums(mate * mine, s).astype(BF16)
            mate_copy(s).start()

        @pl.when(core < NC)
        def _():
            own[s] = partial_sums(core * mine, s)

    place_b = {off: (s, i * bz_size) for s, row in enumerate(order) for i, off in enumerate(row[:2])}
    place_a = {row[2]: (s, 2 * bz_size) for s, row in enumerate(order)}

    def load_b(off, i, cols):
        s, start = place_b[off if off in place_b else off + NZ]
        rows = pl.ds(pl.multiple_of(start + i * 16, 16), 16)
        return own[s, rows, cols] + mate_r[s, rows, cols].astype(F32)

    def load_a(off, i, cols):
        s, start = place_a[off if off in place_a else off + NX]
        rows = pl.ds(pl.multiple_of(start + i * 16, 16), 16)
        return own[s, rows, cols] + mate_r[s, rows, cols].astype(F32)

    def loader(ref, me, n):
        def load(off, i, cols):
            block = lax.rem(me + off + n, n)
            return ref[pl.ds(pl.multiple_of(block * size + i * 16, 16), 16), cols]

        return load

    whole = (0, 0, width)
    windows = [(w, w * (width // WINDOWS), width // WINDOWS) for w in range(WINDOWS)]
    ax = [ScatterRing(NX, x, x_device, load_a, ax_size, ax_s, ax_r, ax_ss, ax_rs, w) for w in windows]
    bz = [ScatterRing(NZ, z, z_device, load_b, bz_size, bz_s, bz_r, bz_ss, bz_rs, w) for w in windows]
    az = ScatterRing(NZ, z, z_device, loader(own_a, z, NZ), size, az_s, az_r, az_ss, az_rs, whole)
    bx = ScatterRing(NX, x, x_device, loader(own_b, x, NX), size, bx_s, bx_r, bx_ss, bx_rs, whole)

    def keep(ref):
        def store(i, cols, total):
            ref[pl.ds(pl.multiple_of(i * 16, 16), 16), cols] = total

        return store

    def deliver(base):
        def store(i, cols, total):
            out[pl.ds(pl.multiple_of(base + i * 16, 16), 16), :] = rescale(total).astype(BF16)

        return store

    def each(rings, k):
        for ring in rings:
            ring.step(k)

    base_a = core * mine
    base_b = base_a + part
    sums(0)
    sums(1)
    mate_copy(0).wait_recv()
    each(bz, 4)
    each(ax, 2)
    sums(2)
    mate_copy(1).wait_recv()
    sums(3)
    each(bz, 3)
    mate_copy(2).wait_recv()
    each(ax, 1)
    mate_copy(3).wait_recv()
    each(bz, 2)
    each(bz, 1)
    for ring in ax:
        ring.finish(keep(own_a))
    az.step(4)
    for ring in bz:
        ring.finish(keep(own_b))
    bx.step(2)
    az.step(3)
    bx.step(1)
    az.step(2)
    bx.finish(deliver(base_b + z * bz_size + x * size))
    gbx = GatherRing(NX, x, x_device, base_b + z * bz_size, size, out, gbx_ss, gbx_rs, whole)
    gbx.step(1)
    az.step(1)
    gbx.arrive(1)
    gbx.step(2)
    az.finish(deliver(base_a + x * ax_size + z * size))
    gaz = GatherRing(NZ, z, z_device, base_a + x * ax_size, size, out, gaz_ss, gaz_rs, whole)
    gaz.step(1)

    gax = [GatherRing(NX, x, x_device, base_a, ax_size, out, gax_ss, gax_rs, w) for w in windows]
    gbz = [GatherRing(NZ, z, z_device, base_b, bz_size, out, gbz_ss, gbz_rs, w) for w in windows]
    forwards = []

    def forward(view):
        index = len(forwards)
        copy = remote(view, view, fwd_ss.at[index], fwd_rs.at[index], mate_device)
        copy.start()
        forwards.append(copy)

    def arrived(ring, k):
        ring.arrive(k)
        if k < ring.n // 2:
            ring.step(k + 1)
        for d in range(2):
            forward(ring.view(ring.source(d, k), ring.cols(d, k)))

    gbx.arrive(2)
    each(gbz, 1)
    forward(gbz[0].view(z, pl.ds(0, width)))
    gaz.arrive(1)
    gaz.step(2)
    gaz.arrive(2)
    gaz.step(3)
    arrived(gbz[0], 1)
    gaz.arrive(3)
    gaz.step(4)
    for ring in gbz[1:]:
        arrived(ring, 1)
    gaz.arrive(4)
    each(gax, 1)
    forward(gax[0].view(x, pl.ds(0, width)))
    for rings, k in ((gbz, 2), (gax, 1), (gbz, 3), (gax, 2), (gbz, 4)):
        for ring in rings:
            arrived(ring, k)
    for copy in forwards:
        copy.wait_recv()
    for copy in ups + forwards + [mate_copy(s) for s in range(4)]:
        copy.wait_send()
    for ring in ax + bz + [az, bx, gbx, gaz] + gax + gbz:
        ring.drain()


def per_device(embeddings, centres):
    rows, width = embeddings.shape
    protos = centres.shape[0]
    mine = protos // 2
    part = mine // 2
    ax_size, bz_size = part // NX, part // NZ
    size = part // (NX * NZ)
    rings = [(NX, ax_size), (NZ, size), (NZ, bz_size), (NX, size)]
    scratch = [
        VMEM((rows, width), BF16),
        VMEM((protos, width), BF16),
        VMEM((NY, rows, width), BF16),
        VMEM((NY, protos, rows), F32),
        VMEM((protos, 128), F32),
        VMEM((protos, 128), F32),
        VMEM((8, 128), F32),
        VMEM((ITERS, 4, protos // 128, 128), F32),
        VMEM((ITERS, protos // 128, 128), F32),
        VMEM((ITERS, NX - 1, protos // 128, 128), F32),
        VMEM((ITERS, NZ - 1, protos // 128, 128), F32),
        VMEM((ITERS, 8, 128), F32),
        VMEM((ITERS, NY - 1, 8, 128), F32),
        VMEM((4, mine // 4, width), BF16),
        VMEM((4, mine // 4, width), BF16),
        VMEM((4, mine // 4, width), F32),
        VMEM((ax_size, width), F32),
        VMEM((bz_size, width), F32),
    ]
    for n, block in rings:
        scratch += [VMEM((2, n // 2, block, width), BF16)] * 2
    pairs = [(6,), (ITERS, 1 + NX - 1 + NZ - 1), (ITERS, NY - 1), (4,)]
    counts = [WINDOWS, 1, WINDOWS, 1]
    pairs += [(w, 2, n // 2) for (n, _), w in zip(rings, counts)]
    pairs += [(1, 2, NZ // 2), (WINDOWS, 2, NX // 2), (1, 2, NX // 2), (WINDOWS, 2, NZ // 2)]
    pairs += [(2 + WINDOWS * (NX + NZ),)]
    scratch += [DMA((2,))]
    for shape in pairs:
        scratch += [DMA(shape)] * 2
    return pl.pallas_call(
        kernel,
        out_shape=VMEM((protos, width), BF16),
        in_specs=[pl.BlockSpec(memory_space=pltpu.HBM)] * 2,
        out_specs=pl.BlockSpec(memory_space=pltpu.VMEM),
        scratch_shapes=scratch,
        compiler_params=pltpu.CompilerParams(
            collective_id=0, has_side_effects=True, vmem_limit_bytes=56 * 1024 * 1024
        ),
    )(embeddings, centres)


def solution(mesh):
    return jax.shard_map(
        per_device,
        mesh=mesh,
        in_specs=(P(("dp", "proto"), None), P("proto", None)),
        out_specs=P("proto", None),
        check_vma=False,
    )
```
